256 devices in a mesh: row: 16 (over z_lo, x), col: 16 (over y, z_hi, core).
Axes of the slice: x: 4, y: 4, z: 8 (z_hi: 2, z_lo: 4; z = z_hi * 4 + z_lo), core: 2. Of those that a mesh axis runs over, the one named last changes fastest.
Arguments:
- inverse_block: bfloat16 [10240, 10240], P('row', 'col'), may hold values from -6 to 6
- factor_cols: bfloat16 [10240, 4096], P('row', 'col'), may hold values from -0.078125 to 0.078125
- diag_inverse: float32 [16, 256, 256], P('col', 'row'), may hold values from -6 to 6
- fill_mask: int32 [40, 16], replicated, may hold values from 0 to 1
Outputs:
- inverse_cols: bfloat16 [10240, 4096], P('row', 'col')
- inverse_diag: float32 [16, 256, 256], P('col', 'row')
The draws below stay inside these ranges and needn't reach their ends.
All inputs are finite; a program needn't handle non-finite values.
Results may differ from the reference program's by a relative error of at most 0.0027.
Values may be sent and summed in bfloat16 or wider, within the bound.
No kernel may reach another device: no remote copies, remote signals or barrier semaphores. Data moves between devices by JAX's collectives and lax.ppermute only.
A program may use at most 64 MiB of HBM per device.

```python
import jax
import jax.numpy as jnp
from jax import lax

W = 256
NBLK = 40
ORDER = 10240
SUPERNODES = 16
N_COL = 16


def draw_fill_mask(key, part):
    scores = jax.random.randint(key, (NBLK, SUPERNODES), 0, NBLK)
    levels = lax.broadcasted_iota(jnp.int32, (NBLK, SUPERNODES), 0)
    return (scores <= levels + NBLK // 4).astype(jnp.int32)


def block_scale(key, shape, pieces, least, high):
    level = 1.0
    for position, blocks in pieces:
        steps = jax.random.uniform(jax.random.fold_in(jax.random.fold_in(key, 6), position), (blocks,), jnp.float32, least / len(pieces), high / len(pieces))
        level = level * jnp.repeat(jnp.exp(steps), shape[position] // blocks).reshape((-1,) + (1,) * (len(shape) - 1 - position))
    return level


def noise(key, shape, scale, bound, pieces=(), held_as=jnp.bfloat16):
    values = scale * jax.random.normal(key, shape, jnp.float32)
    if pieces:
        values = values * block_scale(key, shape, pieces, -0.22, 0.18)
    return jnp.clip(values, -bound, bound).astype(held_as)


def setup_inputs(seed: int = 0) -> dict:
    key_of = jax.random.split(jax.random.key(seed), 5)
    return {
        "inverse_block": noise(key_of[0], (ORDER, ORDER), 1.0, 6.0, ((0, 16), (1, 16))),
        "factor_cols": noise(key_of[1], (ORDER, SUPERNODES * W), (ORDER // 2) ** -0.5, 0.078125, ((0, 16), (1, 16))),
        "diag_inverse": noise(key_of[2], (SUPERNODES, W, W), 1.0, 6.0, ((0, 16), (1, 16)), jnp.float32),
        "fill_mask": draw_fill_mask(jax.random.fold_in(key_of[4], 71), 0),
    }


def build_mask(fill_mask):
    block_count, node_count = fill_mask.shape
    expanded = jnp.broadcast_to(fill_mask[:, None, :], (block_count, W, node_count)).reshape(block_count * W, node_count)
    wide = jnp.broadcast_to(expanded[:, :, None], (block_count * W, node_count, W))
    return wide.reshape(block_count * W, node_count * W)


def reference(inverse_block, factor_cols, diag_inverse, fill_mask):
    column_mask = build_mask(fill_mask)
    selected = factor_cols * column_mask.astype(jnp.bfloat16)
    block_width = ORDER // N_COL

    def add_block(index, running):
        start = (index * block_width).astype(jnp.int32)
        inverse_piece = lax.dynamic_slice_in_dim(inverse_block, start, block_width, 1)
        factor_rows = lax.dynamic_slice_in_dim(selected, start, block_width, 0)
        product = jnp.dot(inverse_piece, factor_rows, preferred_element_type=jnp.float32)
        return running + product

    initial = jnp.zeros((ORDER, selected.shape[1]), jnp.float32)
    summed = lax.fori_loop(jnp.int32(0), jnp.int32(N_COL), add_block, initial)
    inverse_cols = (-summed * column_mask.astype(jnp.float32)).astype(jnp.bfloat16)
    node_count = fill_mask.shape[1]
    left_side = selected.astype(jnp.float32).reshape(ORDER, node_count, W)
    right_side = inverse_cols.astype(jnp.float32).reshape(ORDER, node_count, W)
    correction = jnp.einsum("isa,isb->sab", left_side, right_side)
    inverse_diag = diag_inverse - correction
    return inverse_cols, inverse_diag
```

```python
import jax
import jax.numpy as jnp
from jax import lax
from jax.sharding import Mesh, PartitionSpec as P

AXES = ("zl", "x", "y", "zh", "core")
SIZES = (4, 4, 4, 2, 2)


def _places():
    for zl in range(4):
        for x in range(4):
            for y in range(4):
                for zh in range(2):
                    for core in range(2):
                        yield zl, x, y, zh, core


def _index(place):
    out = 0
    for value, size in zip(place, SIZES):
        out = out * size + value % size
    return out


def _move(value, target, senders=None):
    pairs = [
        (_index(p), _index(target(*p)))
        for p in _places()
        if senders is None or senders(*p)
    ]
    return lax.ppermute(value, AXES, pairs)


def _matched(zl, x, y, zh, core):
    return x % 2 == core


def body(inverse_block, factor_cols, diag_inverse, fill_mask):
    rows, cols = factor_cols.shape
    zl, x, y, zh, core = (lax.axis_index(a) for a in AXES)
    row = zl * 4 + x
    col = y * 4 + zh * 2 + core

    halves = jnp.repeat(fill_mask, 2, axis=0)
    pieces = rows // 128
    mask = lax.dynamic_slice(halves, (row * pieces, col), (pieces, 1)).reshape(pieces, 1, 1)

    own = inverse_block
    far = _move(own, lambda zl, x, y, zh, c: (zl, x, y, zh + 1, c))

    def along_y(v):
        return [
            v,
            _move(v, lambda zl, x, y, zh, c: (zl, x, y - 1, zh, c)),
            _move(v, lambda zl, x, y, zh, c: (zl, x, y + 2, zh, c)),
            _move(v, lambda zl, x, y, zh, c: (zl, x, y + 1, zh, c)),
        ]

    near_blocks = along_y(own)
    far_blocks = along_y(far)

    selected = (factor_cols.reshape(pieces, 128, cols) * mask.astype(jnp.bfloat16)).reshape(rows, cols)
    other = _move(selected, lambda zl, x, y, zh, c: (zl, x, y, zh, 1 - c),
                  lambda zl, x, y, zh, c: x % 2 != c)
    both = jnp.concatenate([selected, other], axis=1)
    line = [
        _move(both, lambda zl, x, y, zh, c, d=d: (zl - d, x, y, zh, c), _matched)
        for d in (1, 2, 3)
    ]

    is_matched = (x % 2) == core

    def along_x(v):
        right = _move(v, lambda zl, x, y, zh, c: (zl, x + 1, y, zh, c), _matched)
        left = _move(v, lambda zl, x, y, zh, c: (zl, x - 1, y, zh, c), _matched)
        across = _move(v, lambda zl, x, y, zh, c: (zl, x + 2, y, zh, c), _matched)
        return jnp.stack([jnp.where(is_matched, v, right), jnp.where(is_matched, across, left)])

    first = along_x(both[None])
    rest = along_x(jnp.stack(line))
    panel = jnp.concatenate([first, rest], axis=1)

    base_x = jnp.where(is_matched, x, (x + 3) % 4) // 2
    total = None
    for away, blocks in ((0, near_blocks), (1, far_blocks)):
        which = ((zh + away) % 2 != base_x).astype(jnp.int32)
        for step, block in enumerate(blocks):
            place = (y + step - zl) % 4
            piece = lax.dynamic_slice(panel, (which, place, 0, 0), (1, 1, rows, 2 * cols))
            product = jnp.dot(block, piece.reshape(rows, 2 * cols), preferred_element_type=jnp.float32)
            total = product if total is None else total + product

    theirs = _move(total[:, cols:], lambda zl, x, y, zh, c: (zl, x, y, zh, 1 - c))
    summed = (total[:, :cols] + theirs).reshape(pieces, 128, cols)
    inverse_cols = (-summed * mask.astype(jnp.float32)).astype(jnp.bfloat16).reshape(rows, cols)

    part = jnp.einsum("ia,ib->ab", selected, inverse_cols, preferred_element_type=jnp.float32)
    shares = lax.all_to_all(part.reshape(16, cols // 16, cols), ("zl", "x"), 0, 0)
    inverse_diag = diag_inverse - jnp.sum(shares, axis=0)[None]
    return inverse_cols, inverse_diag


def solution(mesh):
    fine = Mesh(mesh.devices.reshape(SIZES), AXES)
    row, col = ("zl", "x"), ("y", "zh", "core")
    return jax.shard_map(
        body,
        mesh=fine,
        in_specs=(P(row, col), P(row, col), P(col, row, None), P()),
        out_specs=(P(row, col), P(col, row, None)),
        check_vma=False,
    )
```

```python
import jax
import jax.numpy as jnp
from jax import lax
from jax.sharding import Mesh, PartitionSpec as P


AXES = ("zl", "x", "y", "zh", "core")
SIZES = (4, 4, 4, 2, 2)


def _places():
    for zl in range(4):
        for x in range(4):
            for y in range(4):
                for zh in range(2):
                    for core in range(2):
                        yield zl, x, y, zh, core


def _index(place):
    out = 0
    for value, size in zip(place, SIZES):
        out = out * size + value % size
    return out


def _move(value, target, senders=None):
    pairs = [
        (_index(p), _index(target(*p)))
        for p in _places()
        if senders is None or senders(*p)
    ]
    return lax.ppermute(value, AXES, pairs)


def _matched(zl, x, y, zh, core):
    return x % 2 == core


def body(inverse_block, factor_cols, diag_inverse, fill_mask):
    rows, cols = factor_cols.shape
    zl, x, y, zh, core = (lax.axis_index(a) for a in AXES)
    row = zl * 4 + x
    col = y * 4 + zh * 2 + core

    halves = jnp.repeat(fill_mask, 2, axis=0)
    pieces = rows // 128
    mask = lax.dynamic_slice(halves, (row * pieces, col), (pieces, 1)).reshape(pieces, 1, 1)

    own = inverse_block
    far = _move(own, lambda zl, x, y, zh, c: (zl, x, y, zh + 1, c))

    def along_y(v):
        return jnp.stack([
            v,
            _move(v, lambda zl, x, y, zh, c: (zl, x, y - 1, zh, c)),
            _move(v, lambda zl, x, y, zh, c: (zl, x, y + 2, zh, c)),
            _move(v, lambda zl, x, y, zh, c: (zl, x, y + 1, zh, c)),
        ])

    near_blocks = along_y(own)
    far_blocks = along_y(far)

    selected = (factor_cols.reshape(pieces, 128, cols) * mask.astype(jnp.bfloat16)).reshape(rows, cols)
    other = _move(selected, lambda zl, x, y, zh, c: (zl, x, y, zh, 1 - c),
                  lambda zl, x, y, zh, c: x % 2 != c)
    line = [jnp.concatenate([selected, other], axis=1)]
    for d in (1, 2, 3):
        line.append(_move(line[0], lambda zl, x, y, zh, c: (zl - d, x, y, zh, c), _matched))

    is_matched = (x % 2) == core
    first_near = (jnp.where(is_matched, x, (x + 3) % 4) // 2) == zh
    total = None
    for d, v in enumerate(line):
        right = _move(v, lambda zl, x, y, zh, c: (zl, x + 1, y, zh, c), _matched)
        left = _move(v, lambda zl, x, y, zh, c: (zl, x - 1, y, zh, c), _matched)
        across = _move(v, lambda zl, x, y, zh, c: (zl, x + 2, y, zh, c), _matched)
        if total is not None:
            total, right, left, across = lax.optimization_barrier((total, right, left, across))
        first = jnp.where(is_matched, v, right)
        second = jnp.where(is_matched, across, left)
        place = (zl + d - y) % 4
        for blocks, piece in (
            (near_blocks, jnp.where(first_near, first, second)),
            (far_blocks, jnp.where(first_near, second, first)),
        ):
            block = lax.dynamic_index_in_dim(blocks, place, 0, keepdims=False)
            product = jnp.dot(block, piece, preferred_element_type=jnp.float32)
            total = product if total is None else total + product

    theirs = _move(total[:, cols:], lambda zl, x, y, zh, c: (zl, x, y, zh, 1 - c))
    summed = (total[:, :cols] + theirs).reshape(pieces, 128, cols)
    inverse_cols = (-summed * mask.astype(jnp.float32)).astype(jnp.bfloat16).reshape(rows, cols)

    part = jnp.einsum("ia,ib->ab", selected, inverse_cols, preferred_element_type=jnp.float32)
    shares = lax.all_to_all(part.reshape(16, cols // 16, cols), ("zl", "x"), 0, 0)
    inverse_diag = diag_inverse - jnp.sum(shares, axis=0)[None]
    return inverse_cols, inverse_diag


def solution(mesh):
    fine = Mesh(mesh.devices.reshape(SIZES), AXES)
    row, col = ("zl", "x"), ("y", "zh", "core")
    return jax.shard_map(
        body,
        mesh=fine,
        in_specs=(P(row, col), P(row, col), P(col, row, None), P()),
        out_specs=(P(row, col), P(col, row, None)),
        check_vma=False,
    )
```

```python
import jax
import jax.numpy as jnp
from jax import lax
from jax.sharding import Mesh, PartitionSpec as P


AXES = ("zl", "x", "y", "zh", "core")
SIZES = (4, 4, 4, 2, 2)
PASSED = ('ay',)
KEPT = (1, 2, 3)
DOTS = (('n', 0), ('n', 1), ('n', 3), ('f', 0), ('f', 1), ('f', 3), ('n', 2), ('f', 2))


def _places():
    for zl in range(4):
        for x in range(4):
            for y in range(4):
                for zh in range(2):
                    for core in range(2):
                        yield zl, x, y, zh, core


def _index(place):
    out = 0
    for value, size in zip(place, SIZES):
        out = out * size + value % size
    return out


def _move(value, target, senders=None):
    pairs = [
        (_index(p), _index(target(*p)))
        for p in _places()
        if senders is None or senders(*p)
    ]
    return lax.ppermute(value, AXES, pairs)


def _matched(zl, x, y, zh, core):
    return x % 2 == core


def _unmatched(zl, x, y, zh, core):
    return x % 2 != core


def body(inverse_block, factor_cols, diag_inverse, fill_mask):
    rows, cols = factor_cols.shape
    zl, x, y, zh, core = (lax.axis_index(a) for a in AXES)
    row = zl * 4 + x
    col = y * 4 + zh * 2 + core
    pieces = rows // 128

    halves = jnp.repeat(fill_mask, 2, axis=0)
    mask = lax.dynamic_slice(halves, (row * pieces, col), (pieces, 1)).reshape(pieces, 1, 1)

    def along_y(name, v):
        left = _move(v, lambda zl, x, y, zh, c: (zl, x, y - 1, zh, c))
        if name in PASSED:
            across = _move(left, lambda zl, x, y, zh, c: (zl, x, y - 1, zh, c))
        else:
            across = _move(v, lambda zl, x, y, zh, c: (zl, x, y + 2, zh, c))
        right = _move(v, lambda zl, x, y, zh, c: (zl, x, y + 1, zh, c))
        return jnp.stack([v, left, across, right])

    across_z = lambda zl, x, y, zh, c: (zl, x, y, zh + 1, c)
    near_blocks = along_y("ay", inverse_block)
    far = _move(inverse_block, across_z, _unmatched) + _move(inverse_block, across_z, _matched)
    far_blocks = along_y("by", far)

    selected = (factor_cols.reshape(pieces, 128, cols) * mask.astype(jnp.bfloat16)).reshape(rows, cols)
    other = _move(selected, lambda zl, x, y, zh, c: (zl, x, y, zh, 1 - c),
                  lambda zl, x, y, zh, c: x % 2 != c)
    both = jnp.concatenate([selected, other], axis=1)
    is_matched = (x % 2) == core
    first_near = (jnp.where(is_matched, x, (x + 3) % 4) // 2) == zh
    pairs = []
    for d in range(4):
        v = both
        if d:
            v = _move(both, lambda zl, x, y, zh, c: (zl - d, x, y, zh, c), _matched)
        right = _move(v, lambda zl, x, y, zh, c: (zl, x + 1, y, zh, c), _matched)
        left = _move(v, lambda zl, x, y, zh, c: (zl, x - 1, y, zh, c), _matched)
        if f"r{d}" in PASSED:
            across = _move(right, lambda zl, x, y, zh, c: (zl, x + 1, y, zh, c), _unmatched)
        elif f"l{d}" in PASSED:
            across = _move(left, lambda zl, x, y, zh, c: (zl, x - 1, y, zh, c), _unmatched)
        else:
            across = _move(v, lambda zl, x, y, zh, c: (zl, x + 2, y, zh, c), _matched)
        if d in KEPT:
            v = lax.optimization_barrier(jnp.where(is_matched, v, jnp.zeros_like(v)))
        pairs.append((v, right, left, across))

    total = None
    for near, d in DOTS:
        parts = pairs[d]
        if total is not None:
            total, *parts = lax.optimization_barrier((total, *parts))
        v, right, left, across = parts
        first = jnp.where(is_matched, v, right)
        second = jnp.where(is_matched, across, left)
        piece = jnp.where(first_near == (near == "n"), first, second)
        stack = near_blocks if near == "n" else far_blocks
        block = lax.dynamic_index_in_dim(stack, (zl + d - y) % 4, 0, keepdims=False)
        product = jnp.dot(block, piece, preferred_element_type=jnp.float32)
        total = product if total is None else total + product

    theirs = _move(total[:, cols:], lambda zl, x, y, zh, c: (zl, x, y, zh, 1 - c))
    summed = (total[:, :cols] + theirs).reshape(pieces, 128, cols)
    inverse_cols = (-summed * mask.astype(jnp.float32)).astype(jnp.bfloat16).reshape(rows, cols)

    part = jnp.einsum("ia,ib->ab", selected, inverse_cols, preferred_element_type=jnp.float32)
    shares = lax.all_to_all(part.reshape(16, cols // 16, cols), ("zl", "x"), 0, 0)
    inverse_diag = diag_inverse - jnp.sum(shares, axis=0)[None]
    return inverse_cols, inverse_diag


def solution(mesh):
    fine = Mesh(mesh.devices.reshape(SIZES), AXES)
    row, col = ("zl", "x"), ("y", "zh", "core")
    return jax.shard_map(
        body,
        mesh=fine,
        in_specs=(P(row, col), P(row, col), P(col, row, None), P()),
        out_specs=(P(row, col), P(col, row, None)),
        check_vma=False,
    )
```

```python
import jax
import jax.numpy as jnp
from jax import lax
from jax.sharding import Mesh, PartitionSpec as P


AXES = ("zl", "x", "y", "zh", "core")
SIZES = (4, 4, 4, 2, 2)
PASSED = ('ay',)
KEPT = (2, 3)
DOTS = (('n', 0), ('n', 1), ('n', 3), ('f', 0), ('f', 1), ('f', 3), ('n', 2), ('f', 2))


def _places():
    for zl in range(4):
        for x in range(4):
            for y in range(4):
                for zh in range(2):
                    for core in range(2):
                        yield zl, x, y, zh, core


def _index(place):
    out = 0
    for value, size in zip(place, SIZES):
        out = out * size + value % size
    return out


def _move(value, target, senders=None):
    pairs = [
        (_index(p), _index(target(*p)))
        for p in _places()
        if senders is None or senders(*p)
    ]
    return lax.ppermute(value, AXES, pairs)


def _matched(zl, x, y, zh, core):
    return x % 2 == core


def _unmatched(zl, x, y, zh, core):
    return x % 2 != core


def body(inverse_block, factor_cols, diag_inverse, fill_mask):
    rows, cols = factor_cols.shape
    zl, x, y, zh, core = (lax.axis_index(a) for a in AXES)
    row = zl * 4 + x
    col = y * 4 + zh * 2 + core
    pieces = rows // 128

    halves = jnp.repeat(fill_mask, 2, axis=0)
    mask = lax.dynamic_slice(halves, (row * pieces, col), (pieces, 1)).reshape(pieces, 1, 1)

    def along_y(name, v):
        left = _move(v, lambda zl, x, y, zh, c: (zl, x, y - 1, zh, c))
        if name in PASSED:
            across = _move(left, lambda zl, x, y, zh, c: (zl, x, y - 1, zh, c))
        else:
            across = _move(v, lambda zl, x, y, zh, c: (zl, x, y + 2, zh, c))
        right = _move(v, lambda zl, x, y, zh, c: (zl, x, y + 1, zh, c))
        return jnp.stack([v, left, across, right])

    across_z = lambda zl, x, y, zh, c: (zl, x, y, zh + 1, c)
    near_blocks = along_y("ay", inverse_block)
    from_unmatched = _move(inverse_block, across_z, _unmatched)
    from_matched = _move(inverse_block, across_z, _matched)
    far = jnp.where((x % 2) == core, from_matched, from_unmatched)
    far_blocks = along_y("by", far)

    selected = (factor_cols.reshape(pieces, 128, cols) * mask.astype(jnp.bfloat16)).reshape(rows, cols)
    other = _move(selected, lambda zl, x, y, zh, c: (zl, x, y, zh, 1 - c),
                  lambda zl, x, y, zh, c: x % 2 != c)
    both = jnp.concatenate([selected, other], axis=1)
    is_matched = (x % 2) == core
    first_near = (jnp.where(is_matched, x, (x + 3) % 4) // 2) == zh
    pairs = []
    for d in range(4):
        v = both
        if d:
            v = _move(both, lambda zl, x, y, zh, c: (zl - d, x, y, zh, c), _matched)
        right = _move(v, lambda zl, x, y, zh, c: (zl, x + 1, y, zh, c), _matched)
        left = _move(v, lambda zl, x, y, zh, c: (zl, x - 1, y, zh, c), _matched)
        if f"r{d}" in PASSED:
            across = _move(right, lambda zl, x, y, zh, c: (zl, x + 1, y, zh, c), _unmatched)
        elif f"l{d}" in PASSED:
            across = _move(left, lambda zl, x, y, zh, c: (zl, x - 1, y, zh, c), _unmatched)
        else:
            across = _move(v, lambda zl, x, y, zh, c: (zl, x + 2, y, zh, c), _matched)
        if d in KEPT:
            v = lax.optimization_barrier(jnp.where(is_matched, v, jnp.zeros_like(v)))
        pairs.append((v, right, left, across))

    total = None
    for near, d in DOTS:
        parts = pairs[d]
        if total is not None:
            total, *parts = lax.optimization_barrier((total, *parts))
        v, right, left, across = parts
        first = jnp.where(is_matched, v, right)
        second = jnp.where(is_matched, across, left)
        piece = jnp.where(first_near == (near == "n"), first, second)
        stack = near_blocks if near == "n" else far_blocks
        block = lax.dynamic_index_in_dim(stack, (zl + d - y) % 4, 0, keepdims=False)
        product = jnp.dot(block, piece, preferred_element_type=jnp.float32)
        total = product if total is None else total + product

    theirs = _move(total[:, cols:], lambda zl, x, y, zh, c: (zl, x, y, zh, 1 - c))
    summed = (total[:, :cols] + theirs).reshape(pieces, 128, cols)
    inverse_cols = (-summed * mask.astype(jnp.float32)).astype(jnp.bfloat16).reshape(rows, cols)

    part = jnp.einsum("ia,ib->ab", selected, inverse_cols, preferred_element_type=jnp.float32)
    shares = lax.all_to_all(part.astype(jnp.bfloat16).reshape(16, cols // 16, cols), ("zl", "x"), 0, 0)
    inverse_diag = diag_inverse - jnp.sum(shares.astype(jnp.float32), axis=0)[None]
    return inverse_cols, inverse_diag


def solution(mesh):
    fine = Mesh(mesh.devices.reshape(SIZES), AXES)
    row, col = ("zl", "x"), ("y", "zh", "core")
    return jax.shard_map(
        body,
        mesh=fine,
        in_specs=(P(row, col), P(row, col), P(col, row, None), P()),
        out_specs=(P(row, col), P(col, row, None)),
        check_vma=False,
    )
```
